32 devices in a mesh: row: 4 (over y, core), col: 8 (over z, x).
Axes of the slice: x: 2, y: 2, z: 4, core: 2. Of those that a mesh axis runs over, the one named last changes fastest.
Arguments:
- children: float32 [12288, 6144], P('row', 'col'), may hold values from -6 to 6
- permutation: int32 [12288], replicated, may hold values from 0 to 12287, as said below
- type_counts: int32 [4], replicated, may hold values from 768 to 6144, as said below
- rotation: float32 [12288], replicated, may hold values from -3.140625 to 3.140625
- pole_values: float32 [12288], replicated, may hold values from -0.15 to 12287.15, as said below
- coupling: float32 [12288], replicated, may hold values from -3 to 3, as said below
- root_gap: int32 [2048], replicated, may hold values from 0 to 6142, as said below
- root_offset: float32 [2048], replicated, may hold values from 0.3 to 0.4
Outputs:
- merged: float32 [2048, 12288], P('col', 'row')
The draws below stay inside these ranges and needn't reach their ends.
Inputs may be any that keep to these rules, and one draw needn't show every extreme that they name: A permutation of 0 to 12287. permutation[j] < 6144 for j < type_counts[0] + type_counts[1]; permutation[j] >= 6144 for type_counts[0] + type_counts[1] <= j < live; for every dense joint column j, the value permutation[j] + 6144 stands at some deflated position. The four counts sum to 12288; type_counts[1] lies in 768 to 1536; the smaller of type_counts[0] and type_counts[2] equals 1536; the larger of type_counts[0] + type_counts[1] and type_counts[1] + type_counts[2] equals 4608; type_counts[3] equals 6144. pole_values[j] lies within 0.15 of j. `coupling`: every entry has magnitude 0.3 or more. `root_gap`: distinct values.
All inputs are finite; a program needn't handle non-finite values.
Results may differ from the reference program's by a relative error of at most 0.00007.
Values sent between devices are 32-bit elements; how exact they have to be, the bound alone decides.
A program may use at most 128 MiB of HBM per device.

```python
import jax
import jax.numpy as jnp
from jax import lax

N = 12288
HALF = 6144
ROOTS = 2048


def deflation_plan(key):
    key_list = jax.random.split(jax.random.fold_in(key, 11), 5)
    half_size = N // 2
    dense_count = jax.random.randint(key_list[0], (), N // 16, N // 8 + 1, dtype=jnp.int32)
    busy_count = 3 * N // 8 - dense_count
    other_count = jnp.int32(N // 8)
    flip_bit = jax.random.randint(key_list[2], (), 0, 2, dtype=jnp.int32)
    upper_only = jnp.where(flip_bit == 1, busy_count, other_count)
    lower_count = jnp.where(flip_bit == 1, other_count, busy_count)
    deflated_count = N - upper_only - dense_count - lower_count
    order_top = jax.random.permutation(key_list[3], half_size).astype(jnp.int32)
    rank_top = jnp.argsort(order_top, stable=True).astype(jnp.int32)
    paired = (rank_top >= upper_only) & (rank_top < upper_only + dense_count)
    scores = paired.astype(jnp.int32) * half_size + jax.random.permutation(key_list[4], half_size).astype(jnp.int32)
    order_low = jnp.argsort(scores, stable=True).astype(jnp.int32)
    position = jnp.arange(N, dtype=jnp.int32)
    upper_count = upper_only + dense_count
    live_count = upper_count + lower_count
    spare_top = half_size - upper_count
    tail_index = position - live_count
    pick_top = jnp.clip(position, 0, half_size - 1)
    pick_low = jnp.clip(position - upper_count, 0, half_size - 1)
    pick_spare = jnp.clip(upper_count + tail_index, 0, half_size - 1)
    pick_rest = jnp.clip(lower_count + tail_index - spare_top, 0, half_size - 1)
    result = jnp.where(position < upper_count, order_top[pick_top], jnp.where(position < live_count, half_size + order_low[pick_low], jnp.where(tail_index < spare_top, order_top[pick_spare], half_size + order_low[pick_rest])))
    totals = jnp.stack([upper_only, dense_count, lower_count, deflated_count]).astype(jnp.int32)
    return (result.astype(jnp.int32), totals)


def draw_permutation(key, part):
    return deflation_plan(key)[0]


def draw_type_counts(key, part):
    return deflation_plan(key)[1]


def draw_pole_values(key, part):
    key_list = jax.random.split(jax.random.fold_in(key, 23), 2)
    position = jnp.arange(N).astype(jnp.float32)
    jitter = jax.random.uniform(key_list[1], (N,), jnp.float32, -0.15, 0.15)
    return position + jitter


def draw_coupling(key, part):
    key_list = jax.random.split(jax.random.fold_in(key, 37), 2)
    sign_flip = 2.0 * jax.random.bernoulli(key_list[0], 0.5, (N,)).astype(jnp.float32) - 1.0
    magnitude = jnp.exp(jax.random.uniform(key_list[1], (N,), jnp.float32, jnp.log(0.3), jnp.log(3.0)))
    return sign_flip * magnitude


def draw_root_gap(key, part):
    chosen = jax.random.permutation(jax.random.fold_in(key, 5), N // 2 - 1)
    return chosen[:ROOTS].astype(jnp.int32)


def level_of(key, extent, cuts, low, high):
    level = 1.0
    for axis_at, parts in cuts:
        draws = jax.random.uniform(jax.random.fold_in(jax.random.fold_in(key, 6), axis_at), (parts,), jnp.float32, low / len(cuts), high / len(cuts))
        level = level * jnp.repeat(jnp.exp(draws), extent[axis_at] // parts).reshape((-1,) + (1,) * (len(extent) - 1 - axis_at))
    return level


def centred(own_key, extent, deviation, bound, cuts=(), held_as=jnp.bfloat16):
    values = jax.random.normal(own_key, extent, jnp.float32) * deviation
    if len(cuts) > 0:
        values = level_of(own_key, extent, cuts, -0.22, 0.18) * values
    return jnp.clip(values, min=-bound, max=bound).astype(held_as)


def setup_inputs(seed: int = 0) -> dict:
    streams_of = jax.random.split(jax.random.key(seed), 9)
    return {
        "children": centred(streams_of[0], (N, HALF), 1.0, 6.0, ((0, 4), (1, 8)), jnp.float32),
        "permutation": draw_permutation(jax.random.fold_in(streams_of[8], 71), 0),
        "type_counts": draw_type_counts(jax.random.fold_in(streams_of[8], 71), 0),
        "rotation": jnp.clip(jax.random.uniform(streams_of[3], (N,), jnp.float32, -3.140625, 3.140625), -3.140625, 3.140625),
        "pole_values": draw_pole_values(jax.random.fold_in(streams_of[8], 71), 0),
        "coupling": draw_coupling(jax.random.fold_in(streams_of[8], 71), 0),
        "root_gap": draw_root_gap(jax.random.fold_in(streams_of[8], 71), 0),
        "root_offset": jnp.clip(jax.random.uniform(streams_of[7], (ROOTS,), jnp.float32, 0.3, 0.4), 0.3, 0.4),
    }


EPSILON = 1e-06
EXACT = lax.Precision.HIGHEST

def reference(children, permutation, type_counts, rotation, pole_values, coupling, root_gap, root_offset):
    half_size = N // 2
    joint_index = jnp.arange(N, dtype=jnp.int32)
    upper_end = type_counts[0]
    dense_end = type_counts[0] + type_counts[1]
    live_count = dense_end + type_counts[2]
    source = jnp.where(permutation >= half_size, permutation - half_size, permutation).astype(jnp.int32)
    paired = (joint_index >= upper_end) & (joint_index < dense_end)
    lower_only = (joint_index >= dense_end) & (joint_index < live_count)
    zero_fill = jnp.zeros_like(rotation)
    one_fill = jnp.ones_like(rotation)
    upper_factor = jnp.where(joint_index < upper_end, one_fill, jnp.where(paired, jnp.cos(rotation), zero_fill))
    lower_factor = jnp.where(paired, jnp.sin(rotation), jnp.where(lower_only, one_fill, zero_fill))
    base_poles = pole_values[root_gap]
    gap_diff = pole_values[:, None] - base_poles[None, :] - root_offset[None, :]
    cauchy = coupling[:, None] / gap_diff
    cauchy = jnp.where((joint_index < live_count)[:, None], cauchy, jnp.zeros_like(cauchy))
    norm_values = jnp.sqrt(lax.optimization_barrier(jnp.sum(cauchy * cauchy, axis=0)) + EPSILON)
    unit_cauchy = cauchy / norm_values[None, :]
    upper_rows = children[:half_size][:, source] * upper_factor[None, :]
    merged_upper = lax.dot_general(unit_cauchy, upper_rows, (((0,), (1,)), ((), ())), precision=EXACT, preferred_element_type=jnp.float32)
    lower_rows = children[half_size:][:, source] * lower_factor[None, :]
    merged_lower = lax.dot_general(unit_cauchy, lower_rows, (((0,), (1,)), ((), ())), precision=EXACT, preferred_element_type=jnp.float32)
    return jnp.concatenate([merged_upper, merged_lower], axis=1)
```

```python
import math

import jax
import jax.numpy as jnp
from jax import lax
from jax.sharding import PartitionSpec as P

EPSILON = 1e-06
SPLIT = lax.Precision.HIGH
CHUNKS = 6


def grid_of(groups):
    x_size = 1
    while x_size * x_size * 4 <= groups and groups % (x_size * 2) == 0:
        x_size *= 2
    return groups // x_size, x_size


def joint_keys(permutation, type_counts, rotation, is_upper):
    order_size = permutation.shape[0]
    half_size = order_size // 2
    joint_index = jnp.arange(order_size, dtype=jnp.int32)
    upper_end = type_counts[0]
    dense_end = type_counts[0] + type_counts[1]
    live_count = dense_end + type_counts[2]
    paired = (joint_index >= upper_end) & (joint_index < dense_end)
    upper_only = joint_index < upper_end
    lower_only = (joint_index >= dense_end) & (joint_index < live_count)
    source = jnp.where(permutation >= half_size, permutation - half_size, permutation)
    angle_part = jnp.where(is_upper, jnp.cos(rotation), jnp.sin(rotation))
    factor = jnp.where(paired, angle_part, jnp.ones_like(rotation))
    feeds = paired | jnp.where(is_upper, upper_only, lower_only)
    return jnp.where(feeds, source, -1), factor, joint_index < live_count


def per_device(
    children, permutation, type_counts, rotation, pole_values, coupling, root_gap, root_offset
):
    rows_dev, columns_dev = children.shape
    groups = lax.axis_size("col")
    z_size, x_size = grid_of(groups)
    position = lax.axis_index("col")
    z_at, x_at = position // x_size, position % x_size
    is_upper = lax.axis_index("row") < lax.axis_size("row") // 2
    root_share = root_gap.shape[0] // groups

    chunks = math.gcd(CHUNKS, rows_dev // 128)
    chunk_rows = rows_dev // chunks
    own = [children[c * chunk_rows : (c + 1) * chunk_rows] for c in range(chunks)]
    others = []
    for c in range(chunks):
        got = []
        for shift in range(1, x_size):
            pairs = [
                (z * x_size + x, z * x_size + (x + shift) % x_size)
                for z in range(z_size)
                for x in range(x_size)
            ]
            got.append(lax.ppermute(own[c], "col", pairs))
        others.append(got)

    keys, factor, live = joint_keys(permutation, type_counts, rotation, is_upper)
    scaled = coupling * factor

    gap_blocks = lax.dynamic_index_in_dim(
        root_gap.reshape(z_size, x_size, root_share), x_at, 1, keepdims=False
    )
    offset_blocks = lax.dynamic_index_in_dim(
        root_offset.reshape(z_size, x_size, root_share), x_at, 1, keepdims=False
    )
    base_blocks = pole_values[gap_blocks.reshape(-1)].reshape(z_size, root_share)

    base_all = base_blocks.reshape(-1)
    offset_all = offset_blocks.reshape(-1)

    weights = []
    for shift in range(x_size):
        place = z_at * x_size + (x_at - shift) % x_size
        columns = place * columns_dev + jnp.arange(columns_dev, dtype=jnp.int32)
        hits = keys[None, :] == columns[:, None]
        zero = jnp.float32(0)
        poles = jnp.sum(jnp.where(hits, pole_values[None, :], zero), axis=1)
        numerator = jnp.sum(jnp.where(hits, scaled[None, :], zero), axis=1)
        poles, numerator = lax.optimization_barrier((poles, numerator))
        gap_diff = poles[None, :] - base_all[:, None] - offset_all[:, None]
        weights.append(
            jnp.where(numerator[None, :] != 0, numerator[None, :] / gap_diff, zero)
        )
    weights = lax.optimization_barrier(weights)

    base_own = lax.dynamic_index_in_dim(base_blocks, z_at, 0, keepdims=False)
    offset_own = lax.dynamic_index_in_dim(offset_blocks, z_at, 0, keepdims=False)
    numer = jnp.where(live, coupling, jnp.zeros_like(coupling))
    entries = numer[None, :] / (pole_values[None, :] - base_own[:, None] - offset_own[:, None])
    scale = lax.rsqrt(jnp.sum(entries * entries, axis=1) + EPSILON)

    def product(weight, block):
        return lax.dot_general(
            weight,
            block,
            (((1,), (1,)), ((), ())),
            precision=SPLIT,
            preferred_element_type=jnp.float32,
        )

    outs = []
    for c in range(chunks):
        total = product(weights[0], own[c])
        for shift in range(1, x_size):
            total = total + product(weights[shift], others[c][shift - 1])
        blocks = total.reshape(z_size, root_share, chunk_rows)

        def block_of(index):
            return lax.dynamic_index_in_dim(
                blocks, jnp.clip(index, 0, z_size - 1), 0, keepdims=False
            )

        from_left, from_right = None, None
        for step in range(z_size - 1):
            up = block_of(z_size - 1 - step + z_at)
            down = block_of(z_at - (z_size - 1 - step))
            if from_left is not None:
                up = up + from_left
                down = down + from_right
            senders = range(step + 1)
            from_left = lax.ppermute(
                up,
                "col",
                [
                    (p * x_size + x, (p + 1) * x_size + x)
                    for p in senders
                    for x in range(x_size)
                ],
            )
            from_right = lax.ppermute(
                down,
                "col",
                [
                    ((z_size - 1 - p) * x_size + x, (z_size - 2 - p) * x_size + x)
                    for p in senders
                    for x in range(x_size)
                ],
            )
        mine = block_of(z_at)
        if from_left is not None:
            mine = mine + from_left + from_right
        outs.append(mine * scale[:, None])
    return jnp.concatenate(outs, axis=1)


def solution(mesh):
    placed = (P("row", "col"), P(), P(), P(), P(), P(), P(), P())
    return jax.shard_map(
        per_device, mesh=mesh, in_specs=placed, out_specs=P("col", "row"), check_vma=False
    )
```

```python
import jax
import jax.numpy as jnp
from jax import lax
from jax.sharding import PartitionSpec as P


EPSILON = 1e-06
SPLIT = lax.Precision.HIGH
PARTS = (1, 2, 2, 2, 2, 2, 1)


def grid_of(groups):
    x_size = 1
    while x_size * x_size * 4 <= groups and groups % (x_size * 2) == 0:
        x_size *= 2
    return groups // x_size, x_size


def row_spans(rows):
    unit = rows // sum(PARTS)
    if unit * sum(PARTS) != rows or unit % 128 != 0:
        return [(0, rows)]
    return [(sum(PARTS[:c]) * unit, part * unit) for c, part in enumerate(PARTS)]


def joint_keys(permutation, type_counts, rotation, is_upper):
    order_size = permutation.shape[0]
    half_size = order_size // 2
    joint_index = jnp.arange(order_size, dtype=jnp.int32)
    upper_end = type_counts[0]
    dense_end = type_counts[0] + type_counts[1]
    live_count = dense_end + type_counts[2]
    paired = (joint_index >= upper_end) & (joint_index < dense_end)
    upper_only = joint_index < upper_end
    lower_only = (joint_index >= dense_end) & (joint_index < live_count)
    source = jnp.where(permutation >= half_size, permutation - half_size, permutation)
    angle_part = jnp.where(is_upper, jnp.cos(rotation), jnp.sin(rotation))
    factor = jnp.where(paired, angle_part, jnp.ones_like(rotation))
    feeds = paired | jnp.where(is_upper, upper_only, lower_only)
    return jnp.where(feeds, source, -1), factor, joint_index < live_count


def look_up(table, index):
    rows = table.reshape(-1, 128)
    row_hits = index[:, None] // 128 == jnp.arange(rows.shape[0], dtype=jnp.int32)[None, :]
    picked = lax.dot(row_hits.astype(jnp.float32), rows, precision=lax.Precision.HIGHEST)
    lane_hits = index[:, None] % 128 == jnp.arange(128, dtype=jnp.int32)[None, :]
    return jnp.sum(jnp.where(lane_hits, picked, jnp.zeros_like(picked)), axis=1)


def by_source(keys, values, half_size):
    row_hits = jnp.arange(half_size // 128, dtype=jnp.int32)[:, None] == keys[None, :] // 128
    lane_hits = keys[None, :] % 128 == jnp.arange(128, dtype=jnp.int32)[:, None]
    stacked = jnp.concatenate(
        [jnp.where(row_hits & (keys >= 0)[None, :], value[None, :], 0.0) for value in values]
    )
    placed = lax.dot_general(
        stacked,
        lane_hits.astype(jnp.float32),
        (((1,), (1,)), ((), ())),
        precision=lax.Precision.HIGHEST,
        preferred_element_type=jnp.float32,
    )
    return [part.reshape(-1) for part in jnp.split(placed, len(values))]


def per_device(
    children, permutation, type_counts, rotation, pole_values, coupling, root_gap, root_offset
):
    rows_dev, columns_dev = children.shape
    groups = lax.axis_size("col")
    z_size, x_size = grid_of(groups)
    position = lax.axis_index("col")
    z_at, x_at = position // x_size, position % x_size
    is_upper = lax.axis_index("row") < lax.axis_size("row") // 2
    root_share = root_gap.shape[0] // groups

    spans = row_spans(rows_dev)
    chunks = len(spans)
    own = [children[first : first + count] for first, count in spans]
    others = []
    for c in range(chunks):
        got = []
        for shift in range(1, x_size):
            pairs = [
                (z * x_size + x, z * x_size + (x + shift) % x_size)
                for z in range(z_size)
                for x in range(x_size)
            ]
            got.append(lax.ppermute(own[c], "col", pairs))
        others.append(got)

    keys, factor, live = joint_keys(permutation, type_counts, rotation, is_upper)
    scaled = coupling * factor

    gap_blocks = lax.dynamic_index_in_dim(
        root_gap.reshape(z_size, x_size, root_share), x_at, 1, keepdims=False
    )
    offset_blocks = lax.dynamic_index_in_dim(
        root_offset.reshape(z_size, x_size, root_share), x_at, 1, keepdims=False
    )
    base_blocks = look_up(pole_values, gap_blocks.reshape(-1)).reshape(z_size, root_share)

    base_all = base_blocks.reshape(-1)
    offset_all = offset_blocks.reshape(-1)

    base_all, keys, scaled = lax.optimization_barrier((base_all, keys, scaled))
    all_poles, all_numerators = by_source(keys, (pole_values, scaled), columns_dev * groups)
    zero = jnp.float32(0)
    weights = []
    for shift in range(x_size):
        place = z_at * x_size + (x_at - shift) % x_size
        poles = lax.dynamic_slice_in_dim(all_poles, place * columns_dev, columns_dev)
        numerator = lax.dynamic_slice_in_dim(all_numerators, place * columns_dev, columns_dev)
        gap_diff = poles[None, :] - base_all[:, None] - offset_all[:, None]
        weights.append(
            jnp.where(numerator[None, :] != 0, numerator[None, :] / gap_diff, zero)
        )
    weights = lax.optimization_barrier(weights)

    base_own = lax.dynamic_index_in_dim(base_blocks, z_at, 0, keepdims=False)
    offset_own = lax.dynamic_index_in_dim(offset_blocks, z_at, 0, keepdims=False)
    numer = jnp.where(live, coupling, jnp.zeros_like(coupling))
    entries = numer[None, :] / (pole_values[None, :] - base_own[:, None] - offset_own[:, None])
    scale = lax.rsqrt(jnp.sum(entries * entries, axis=1) + EPSILON)

    def product(weight, block):
        return lax.dot_general(
            weight,
            block,
            (((1,), (1,)), ((), ())),
            precision=SPLIT,
            preferred_element_type=jnp.float32,
        )

    outs = []
    for c in range(chunks):
        total = product(weights[0], own[c])
        for shift in range(1, x_size):
            total = total + product(weights[shift], others[c][shift - 1])
        blocks = total.reshape(z_size, root_share, total.shape[1])

        def block_of(index, blocks=blocks):
            return lax.dynamic_index_in_dim(
                blocks, jnp.clip(index, 0, z_size - 1), 0, keepdims=False
            )

        from_left, from_right = None, None
        for step in range(z_size - 1):
            up = block_of(z_size - 1 - step + z_at)
            down = block_of(z_at - (z_size - 1 - step))
            if from_left is not None:
                up = up + from_left
                down = down + from_right
            senders = range(step + 1)
            from_left = lax.ppermute(
                up,
                "col",
                [(p * x_size + x, (p + 1) * x_size + x) for p in senders for x in range(x_size)],
            )
            from_right = lax.ppermute(
                down,
                "col",
                [
                    ((z_size - 1 - p) * x_size + x, (z_size - 2 - p) * x_size + x)
                    for p in senders
                    for x in range(x_size)
                ],
            )
        mine = block_of(z_at)
        if from_left is not None:
            mine = mine + from_left + from_right
        outs.append(mine * scale[:, None])
    return jnp.concatenate(outs, axis=1)


def solution(mesh):
    placed = (P("row", "col"), P(), P(), P(), P(), P(), P(), P())

    return jax.shard_map(
        per_device, mesh=mesh, in_specs=placed, out_specs=P("col", "row"), check_vma=False
    )
```
